32 devices in a mesh: row: 4 (over y, x), col: 8 (over z, core).
Axes of the slice: x: 2, y: 2, z: 4, core: 2. Of those that a mesh axis runs over, the one named last changes fastest.
Arguments:
- operators: float32 [4, 8, 768, 768], P('row', 'col'), may hold values from -0.1875 to 0.1875
- positions: int32 [4, 8, 256], P('row', 'col'), may hold values from 0 to 767
- amplitudes: float32 [4, 8, 256], P('row', 'col'), may hold values from -96 to 96
Outputs:
- traces: float32 [4, 8, 256, 768], P('row', 'col')
The draws below stay inside these ranges and needn't reach their ends.
All inputs are finite; a program needn't handle non-finite values.
Results may differ from the reference program's by a relative error of at most 0.0003.
Values sent between devices are 32-bit elements; how exact they have to be, the bound alone decides.
A program may use at most 64 MiB of HBM per device.

```python
import jax
import jax.numpy as jnp
from jax import lax

TRACE_ORDER = 768
SHOT_TOTAL = 256
SUBDOMAIN_ROWS = 4
SUBDOMAIN_COLUMNS = 8


def with_ends(values, key, smallest, largest):
    place = [jax.random.randint(jax.random.fold_in(key, axis), (), 0, length) for axis, length in enumerate(values.shape)]
    longest = values.shape.index(max(values.shape))
    next_to = place[:longest] + [(place[longest] + 1) % values.shape[longest]] + place[longest + 1:]
    return values.at[tuple(place)].set(smallest).at[tuple(next_to)].set(largest)


def block_scale(rng, extent, pieces, least, top_value):
    def one(position, blocks):
        heights = jax.random.uniform(jax.random.fold_in(jax.random.fold_in(rng, 6), position), (blocks,), jnp.float32, least / len(pieces), top_value / len(pieces))
        return jnp.repeat(jnp.exp(heights), extent[position] // blocks).reshape((-1,) + (1,) * (len(extent) - position - 1))

    factor_of = one(*pieces[0])
    for cut in pieces[1:]:
        factor_of = factor_of * one(*cut)
    return factor_of


def scatter_about(stream_key, extent, width, bound, pieces=(), held_as=jnp.bfloat16):
    level = block_scale(stream_key, extent, pieces, -0.22, 0.18) if pieces else 1.0
    entries = jax.random.normal(stream_key, extent, jnp.float32) * width * level
    return jnp.minimum(jnp.maximum(entries, -bound), bound).astype(held_as)


def setup_inputs(seed: int = 0) -> dict:
    key_list = jax.random.split(jax.random.key(seed), 4)
    operators = scatter_about(key_list[0], (SUBDOMAIN_ROWS, SUBDOMAIN_COLUMNS, TRACE_ORDER, TRACE_ORDER), (TRACE_ORDER * 5 // 4) ** -0.5, 0.1875, ((0, 4), (1, 8)), jnp.float32)
    positions = with_ends(jax.random.randint(key_list[1], (SUBDOMAIN_ROWS, SUBDOMAIN_COLUMNS, SHOT_TOTAL), 0, TRACE_ORDER), jax.random.fold_in(key_list[1], 1), 0, TRACE_ORDER - 1).astype(jnp.int32)
    amplitudes = scatter_about(key_list[2], (SUBDOMAIN_ROWS, SUBDOMAIN_COLUMNS, SHOT_TOTAL), 16.0, 96.0, ((0, 4), (1, 8)), jnp.float32)
    return dict(operators=operators, positions=positions, amplitudes=amplitudes)


def inject(result, source_at, source_val):
    marked = lax.broadcasted_iota(jnp.int32, result.shape, 1) == source_at[:, None].astype(jnp.int32)
    return result + jnp.where(marked, source_val[:, None], jnp.zeros_like(result))


def sweep_all(matrices, places, strength):
    half_width = matrices.shape[-1] // 2
    shot_count = places.shape[2]

    def row_step(north_traces_full, row_data):
        def cell_step(west_in, cell_data):
            matrix, north_in, source_at, source_val = cell_data
            inputs = jnp.concatenate([north_in, west_in], axis=1)
            product = jnp.dot(inputs, matrix, precision=lax.Precision.HIGHEST, preferred_element_type=jnp.float32)
            result = inject(product, source_at, source_val)
            return result[:, half_width:], (result[:, :half_width], result)

        start_west = jnp.zeros((shot_count, half_width), jnp.float32)
        ignored_slot, (south_all, results) = lax.scan(cell_step, start_west, (row_data[0], north_traces_full, row_data[1], row_data[2]))
        return south_all, results

    start_north = jnp.zeros((places.shape[1], shot_count, half_width), jnp.float32)
    ignored_slot, results = lax.scan(row_step, start_north, (matrices, places, strength))
    return results


def reference(operators, positions, amplitudes):
    forward = sweep_all(operators, positions, amplitudes)
    flipped = jnp.flip(jnp.swapaxes(operators, 2, 3), (0, 1))
    backward = sweep_all(flipped, jnp.flip(positions, (0, 1)), jnp.flip(amplitudes, (0, 1)))
    return forward + jnp.flip(backward, (0, 1))
```

```python
import functools

import jax
import jax.numpy as jnp
from jax import lax
from jax.experimental import pallas as pl
from jax.experimental.pallas import tpu as pltpu
from jax.sharding import PartitionSpec as P

BATCH = 32
CORE_HOP, CHIP_HOP, ROW_HOP, FAR_HOP, PERIOD = 16, 26, 28, 36, 1
MESH = pl.DeviceIdType.MESH


def kernel(
    rows, cols, op_hbm, pos_ref, amp_ref, out_ref,
    op_f32, hi_ref, lo_ref, hi_turned, lo_turned, pos_all, amp_all,
    north_in, west_in, south_in, east_in,
    south_out, east_out, north_out, west_out,
    op_sem, send_sem, recv_sem,
):
    row = lax.axis_index("row")
    col = lax.axis_index("col")
    batches, batch, half = north_in.shape
    order = 2 * half
    has_north, has_south = row > 0, row < rows - 1
    has_west, has_east = col > 0, col < cols - 1

    load = pltpu.make_async_copy(op_hbm.at[0, 0], op_f32, op_sem)
    load.start()

    barrier = pltpu.get_barrier_semaphore()
    sides = (
        (has_north, (row - 1, col)),
        (has_south, (row + 1, col)),
        (has_west, (row, col - 1)),
        (has_east, (row, col + 1)),
    )
    count = 0
    for present, where in sides:
        count = count + present.astype(jnp.int32)

        @pl.when(present)
        def _(where=where):
            pl.semaphore_signal(barrier, inc=1, device_id=where, device_id_type=MESH)

    for present, ref in ((has_north, north_in), (has_west, west_in), (has_south, south_in), (has_east, east_in)):
        @pl.when(jnp.logical_not(present))
        def _(ref=ref):
            ref[...] = jnp.zeros_like(ref)

    shots = batches * batch
    pos_all[...] = jnp.transpose(jnp.broadcast_to(pos_ref[0], (128, shots)))
    amp_all[...] = jnp.transpose(jnp.broadcast_to(amp_ref[0], (128, shots)))

    def split(value, high_ref, low_ref):
        high = value.astype(jnp.bfloat16)
        high_ref[...] = high
        low_ref[...] = (value - high.astype(jnp.float32)).astype(jnp.bfloat16)

    pl.semaphore_wait(barrier, count)

    def link(kind, b):
        src, dst, where = (
            (south_out, north_in, (row + 1, col)),
            (east_out, west_in, (row, col + 1)),
            (north_out, south_in, (row - 1, col)),
            (west_out, east_in, (row, col - 1)),
        )[kind]
        return pltpu.make_async_remote_copy(
            src_ref=src.at[b], dst_ref=dst.at[b],
            send_sem=send_sem.at[kind, b], recv_sem=recv_sem.at[kind, b],
            device_id=where, device_id_type=MESH,
        )

    def product(both, high, adjoint):
        wide, narrow = (hi_turned, lo_turned) if adjoint else (hi_ref, lo_ref)
        first = jnp.dot(both, wide[...], preferred_element_type=jnp.float32)
        second = jnp.dot(high, narrow[...], preferred_element_type=jnp.float32)
        return first[:batch] + (first[batch:] + second)

    def source(b, width, offset):
        at = pl.ds(pl.multiple_of(b * batch, batch), batch)
        spot, strength = pos_all[at, :], amp_all[at, :]
        lanes = lax.broadcasted_iota(jnp.int32, (batch, 128), 1)
        return jnp.concatenate(
            [jnp.where(lanes + (offset + j) == spot, strength, 0.0) for j in range(0, width, 128)], axis=1
        )

    def corner(b, row_out, col_out, put_row, put_col, row_kind, col_kind):
        row_out[b] = source(b, half, 0)
        col_out[b] = source(b, half, half)

        @pl.when(put_row)
        def _():
            link(row_kind, b).start()

        @pl.when(put_col)
        def _():
            link(col_kind, b).start()

    def cell(b, adjoint, row_in, col_in, got_row, got_col, row_out, col_out, put_row, put_col, row_kind, col_kind):
        @pl.when(got_row)
        def _():
            link(row_kind, b).wait_recv()

        @pl.when(got_col)
        def _():
            link(col_kind, b).wait_recv()

        inputs = jnp.concatenate([row_in[b], col_in[b]], axis=1)
        high = inputs.astype(jnp.bfloat16)
        low = (inputs - high.astype(jnp.float32)).astype(jnp.bfloat16)
        both = jnp.concatenate([high, low], axis=0)
        result = product(both, high, adjoint) + source(b, order, 0)
        row_out[b] = result[:, :half]

        @pl.when(put_row)
        def _():
            link(row_kind, b).start()

        col_out[b] = result[:, half:]

        @pl.when(put_col)
        def _():
            link(col_kind, b).start()

    def reach(r, c):
        return (r * ROW_HOP + (r // 2) * (FAR_HOP - ROW_HOP)
                + ((c + 1) // 2) * CORE_HOP + (c // 2) * CHIP_HOP)

    lead_fwd = reach(row, col)
    lead_adj = reach(rows - 1, cols - 1) - lead_fwd
    first_cell = jnp.logical_not(jnp.logical_or(has_north, has_west))
    last_cell = jnp.logical_not(jnp.logical_or(has_south, has_east))

    @pl.when(first_cell)
    def _():
        lax.fori_loop(0, batches, lambda b, carry: (corner(
            b, south_out, east_out, has_south, has_east, 0, 1), carry)[1], 0)

    @pl.when(last_cell)
    def _():
        lax.fori_loop(0, batches, lambda b, carry: (corner(
            b, north_out, west_out, has_north, has_west, 2, 3), carry)[1], 0)

    load.wait()
    split(op_f32[...], hi_ref, lo_ref)
    turn_at = jnp.where(row + col == 1, batches, 0)

    def tick(step, carry):
        fwd, adj = carry
        fwd_next = jnp.logical_and(
            fwd < batches,
            jnp.logical_or(adj >= batches, lead_fwd + fwd * PERIOD <= lead_adj + adj * PERIOD),
        )

        @pl.when(step == turn_at)
        def _():
            split(jnp.transpose(op_f32[...]), hi_turned, lo_turned)

        @pl.when(jnp.logical_and(fwd_next, jnp.logical_not(first_cell)))
        def _():
            cell(fwd, False, north_in, west_in, has_north, has_west,
                 south_out, east_out, has_south, has_east, 0, 1)

        @pl.when(jnp.logical_not(jnp.logical_or(fwd_next, last_cell)))
        def _():
            cell(adj, True, south_in, east_in, has_south, has_east,
                 north_out, west_out, has_north, has_west, 2, 3)

        done = jnp.where(fwd_next, fwd, adj)

        @pl.when(jnp.where(fwd_next, fwd < adj, adj < fwd))
        def _():
            at = pl.ds(pl.multiple_of(done * batch, batch), batch)
            out_ref[0, 0, at, :half] = south_out[done] + north_out[done]
            out_ref[0, 0, at, half:] = east_out[done] + west_out[done]

        moved = fwd_next.astype(jnp.int32)
        return fwd + moved, adj + 1 - moved

    lax.fori_loop(0, 2 * batches, tick, (jnp.int32(0), jnp.int32(0)))

    def drain(b, carry):
        for kind, present in enumerate((has_south, has_east, has_north, has_west)):
            @pl.when(present)
            def _(kind=kind):
                link(kind, b).wait_send()
        return carry

    lax.fori_loop(0, batches, drain, 0)


def local(rows, cols, operators, positions, amplitudes):
    order = operators.shape[-1]
    shots = positions.shape[-1]
    half = order // 2
    batches = shots // BATCH
    slots = pltpu.VMEM((batches, BATCH, half), jnp.float32)
    return pl.pallas_call(
        functools.partial(kernel, rows, cols),
        out_shape=jax.ShapeDtypeStruct((1, 1, shots, order), jnp.float32),
        in_specs=[
            pl.BlockSpec(memory_space=pltpu.HBM),
            pl.BlockSpec(memory_space=pltpu.VMEM),
            pl.BlockSpec(memory_space=pltpu.VMEM),
        ],
        out_specs=pl.BlockSpec(memory_space=pltpu.VMEM),
        scratch_shapes=[
            pltpu.VMEM((order, order), jnp.float32),
            pltpu.VMEM((order, order), jnp.bfloat16),
            pltpu.VMEM((order, order), jnp.bfloat16),
            pltpu.VMEM((order, order), jnp.bfloat16),
            pltpu.VMEM((order, order), jnp.bfloat16),
            pltpu.VMEM((shots, 128), jnp.int32),
            pltpu.VMEM((shots, 128), jnp.float32),
            slots, slots, slots, slots,
            slots, slots, slots, slots,
            pltpu.SemaphoreType.DMA,
            pltpu.SemaphoreType.DMA((4, batches)),
            pltpu.SemaphoreType.DMA((4, batches)),
        ],
        compiler_params=pltpu.CompilerParams(collective_id=0, has_side_effects=True, vmem_limit_bytes=62 << 20),
    )(operators, positions, amplitudes)


def solution(mesh):
    in_specs = (P("row", "col", None, None), P("row", "col", None), P("row", "col", None))
    out_specs = P("row", "col", None, None)
    body = functools.partial(local, mesh.shape["row"], mesh.shape["col"])
    return jax.shard_map(body, mesh=mesh, in_specs=in_specs, out_specs=out_specs, check_vma=False)
```

```python
import functools

import jax
import jax.numpy as jnp
from jax import lax
from jax.experimental import pallas as pl
from jax.experimental.pallas import tpu as pltpu
from jax.sharding import PartitionSpec as P

BATCH = 32
CORE_HOP, CHIP_HOP, ROW_HOP, FAR_HOP, PERIOD = 16, 26, 28, 36, 1
MESH = pl.DeviceIdType.MESH


def kernel(
    rows, cols, op_hbm, pos_ref, amp_ref, out_ref,
    op_f32, hi_ref, lo_ref, hi_turned, lo_turned, pos_all, amp_all,
    north_in, west_in, south_in, east_in,
    south_out, east_out, north_out, west_out,
    op_sem, send_sem, recv_sem,
):
    row = lax.axis_index("row")
    col = lax.axis_index("col")
    batches, batch, half = north_in.shape
    order = 2 * half
    has_north, has_south = row > 0, row < rows - 1
    has_west, has_east = col > 0, col < cols - 1

    load = pltpu.make_async_copy(op_hbm.at[0, 0], op_f32, op_sem)
    load.start()

    barrier = pltpu.get_barrier_semaphore()
    sides = (
        (has_north, (row - 1, col)),
        (has_south, (row + 1, col)),
        (has_west, (row, col - 1)),
        (has_east, (row, col + 1)),
    )
    count = 0
    for present, where in sides:
        count = count + present.astype(jnp.int32)

        @pl.when(present)
        def _(where=where):
            pl.semaphore_signal(barrier, inc=1, device_id=where, device_id_type=MESH)

    for present, ref in ((has_north, north_in), (has_west, west_in), (has_south, south_in), (has_east, east_in)):
        @pl.when(jnp.logical_not(present))
        def _(ref=ref):
            ref[...] = jnp.zeros_like(ref)

    shots = batches * batch
    pos_all[...] = jnp.transpose(jnp.broadcast_to(pos_ref[0], (128, shots)))
    amp_all[...] = jnp.transpose(jnp.broadcast_to(amp_ref[0], (128, shots)))

    def split(value, high_ref, low_ref):
        high = value.astype(jnp.bfloat16)
        high_ref[...] = high
        low_ref[...] = (value - high.astype(jnp.float32)).astype(jnp.bfloat16)

    pl.semaphore_wait(barrier, count)

    def link(kind, b):
        src, dst, where = (
            (south_out, north_in, (row + 1, col)),
            (east_out, west_in, (row, col + 1)),
            (north_out, south_in, (row - 1, col)),
            (west_out, east_in, (row, col - 1)),
        )[kind]
        return pltpu.make_async_remote_copy(
            src_ref=src.at[b], dst_ref=dst.at[b],
            send_sem=send_sem.at[kind, b], recv_sem=recv_sem.at[kind, b],
            device_id=where, device_id_type=MESH,
        )

    def product(both, high, adjoint):
        wide, narrow = (hi_turned, lo_turned) if adjoint else (hi_ref, lo_ref)
        first = jnp.dot(both, wide[...], preferred_element_type=jnp.float32)
        second = jnp.dot(high, narrow[...], preferred_element_type=jnp.float32)
        return first[:batch] + (first[batch:] + second)

    def source(b, width, offset):
        at = pl.ds(pl.multiple_of(b * batch, batch), batch)
        spot, strength = pos_all[at, :], amp_all[at, :]
        lanes = lax.broadcasted_iota(jnp.int32, (batch, 128), 1)
        return jnp.concatenate(
            [jnp.where(lanes + (offset + j) == spot, strength, 0.0) for j in range(0, width, 128)], axis=1
        )

    def corner(b, row_out, col_out, put_row, put_col, row_kind, col_kind):
        row_out[b] = source(b, half, 0)
        col_out[b] = source(b, half, half)

        @pl.when(put_row)
        def _():
            link(row_kind, b).start()

        @pl.when(put_col)
        def _():
            link(col_kind, b).start()

    def cell(b, adjoint, row_in, col_in, got_row, got_col, row_out, col_out, put_row, put_col, row_kind, col_kind):
        @pl.when(got_row)
        def _():
            link(row_kind, b).wait_recv()

        @pl.when(got_col)
        def _():
            link(col_kind, b).wait_recv()

        inputs = jnp.concatenate([row_in[b], col_in[b]], axis=1)
        high = inputs.astype(jnp.bfloat16)
        low = (inputs - high.astype(jnp.float32)).astype(jnp.bfloat16)
        both = jnp.concatenate([high, low], axis=0)
        result = product(both, high, adjoint) + source(b, order, 0)
        row_out[b] = result[:, :half]

        @pl.when(put_row)
        def _():
            link(row_kind, b).start()

        col_out[b] = result[:, half:]

        @pl.when(put_col)
        def _():
            link(col_kind, b).start()

    def reach(r, c):
        return (r * ROW_HOP + (r // 2) * (FAR_HOP - ROW_HOP)
                + ((c + 1) // 2) * CORE_HOP + (c // 2) * CHIP_HOP)

    lead_fwd = reach(row, col)
    lead_adj = reach(rows - 1, cols - 1) - lead_fwd
    first_cell = jnp.logical_not(jnp.logical_or(has_north, has_west))
    last_cell = jnp.logical_not(jnp.logical_or(has_south, has_east))

    @pl.when(first_cell)
    def _():
        lax.fori_loop(0, batches, lambda b, carry: (corner(
            b, south_out, east_out, has_south, has_east, 0, 1), carry)[1], 0)

    @pl.when(last_cell)
    def _():
        lax.fori_loop(0, batches, lambda b, carry: (corner(
            b, north_out, west_out, has_north, has_west, 2, 3), carry)[1], 0)

    load.wait()
    split(op_f32[...], hi_ref, lo_ref)
    turn_at = jnp.where(row + col == 1, batches, 0)

    def tick(step, carry):
        fwd, adj = carry
        fwd_next = jnp.logical_and(
            fwd < batches,
            jnp.logical_or(adj >= batches, lead_fwd + fwd * PERIOD <= lead_adj + adj * PERIOD),
        )

        @pl.when(step == turn_at)
        def _():
            split(jnp.transpose(op_f32[...]), hi_turned, lo_turned)

        @pl.when(jnp.logical_and(fwd_next, jnp.logical_not(first_cell)))
        def _():
            cell(fwd, False, north_in, west_in, has_north, has_west,
                 south_out, east_out, has_south, has_east, 0, 1)

        @pl.when(jnp.logical_not(jnp.logical_or(fwd_next, last_cell)))
        def _():
            cell(adj, True, south_in, east_in, has_south, has_east,
                 north_out, west_out, has_north, has_west, 2, 3)

        done = jnp.where(fwd_next, fwd, adj)

        @pl.when(jnp.where(fwd_next, fwd < adj, adj < fwd))
        def _():
            at = pl.ds(pl.multiple_of(done * batch, batch), batch)
            out_ref[0, 0, at, :half] = south_out[done] + north_out[done]
            out_ref[0, 0, at, half:] = east_out[done] + west_out[done]

        moved = fwd_next.astype(jnp.int32)
        return fwd + moved, adj + 1 - moved

    lax.fori_loop(0, 2 * batches, tick, (jnp.int32(0), jnp.int32(0)))

    def drain(b, carry):
        for kind, present in enumerate((has_south, has_east, has_north, has_west)):
            @pl.when(present)
            def _(kind=kind):
                link(kind, b).wait_send()
        return carry

    lax.fori_loop(0, batches, drain, 0)


def local(rows, cols, operators, positions, amplitudes):
    order = operators.shape[-1]
    shots = positions.shape[-1]
    half = order // 2
    batches = shots // BATCH
    slots = pltpu.VMEM((batches, BATCH, half), jnp.float32)
    return pl.pallas_call(
        functools.partial(kernel, rows, cols),
        out_shape=jax.ShapeDtypeStruct((1, 1, shots, order), jnp.float32),
        in_specs=[
            pl.BlockSpec(memory_space=pltpu.HBM),
            pl.BlockSpec(memory_space=pltpu.VMEM),
            pl.BlockSpec(memory_space=pltpu.VMEM),
        ],
        out_specs=pl.BlockSpec(memory_space=pltpu.VMEM),
        scratch_shapes=[
            pltpu.VMEM((order, order), jnp.float32),
            pltpu.VMEM((order, order), jnp.bfloat16),
            pltpu.VMEM((order, order), jnp.bfloat16),
            pltpu.VMEM((order, order), jnp.bfloat16),
            pltpu.VMEM((order, order), jnp.bfloat16),
            pltpu.VMEM((shots, 128), jnp.int32),
            pltpu.VMEM((shots, 128), jnp.float32),
            slots, slots, slots, slots,
            slots, slots, slots, slots,
            pltpu.SemaphoreType.DMA,
            pltpu.SemaphoreType.DMA((4, batches)),
            pltpu.SemaphoreType.DMA((4, batches)),
        ],
        compiler_params=pltpu.CompilerParams(collective_id=0, has_side_effects=True, vmem_limit_bytes=52 << 20),
    )(operators, positions, amplitudes)


def solution(mesh):
    in_specs = (P("row", "col", None, None), P("row", "col", None), P("row", "col", None))
    out_specs = P("row", "col", None, None)
    body = functools.partial(local, mesh.shape["row"], mesh.shape["col"])
    return jax.shard_map(body, mesh=mesh, in_specs=in_specs, out_specs=out_specs, check_vma=False)
```

```python
import functools

import jax
import jax.numpy as jnp
from jax import lax
from jax.experimental import pallas as pl
from jax.experimental.pallas import tpu as pltpu
from jax.sharding import PartitionSpec as P

BATCH = 32
CORE_HOP, CHIP_HOP, ROW_HOP, FAR_HOP, RELAY_HOP, PERIOD = 15, 32, 36, 50, 27, 5
MESH = pl.DeviceIdType.MESH


def kernel(
    rows, cols, op_hbm, pos_ref, amp_ref, out_ref,
    op_f32, hi_ref, lo_ref, hi_turned, lo_turned, pos_all, amp_all,
    north_in, west_in, south_in, east_in,
    south_out, east_out, north_out, west_out, passing,
    op_sem, send_sem, recv_sem, pass_sem, onward_sem,
):
    row = lax.axis_index("row")
    col = lax.axis_index("col")
    batches, batch, half = north_in.shape
    order = 2 * half
    has_north, has_south = row > 0, row < rows - 1
    has_west, has_east = col > 0, col < cols - 1

    load = pltpu.make_async_copy(op_hbm.at[0, 0], op_f32, op_sem)
    load.start()

    middle, chip = rows // 2, cols // 4
    partner = col + 1 - 2 * (col % 2)
    fwd_zone, adj_zone = col // 2 == chip, col // 2 == chip - 1
    zone = jnp.logical_or(fwd_zone, adj_zone)
    relay_row = jnp.where(fwd_zone, rows - 1, 0)
    from_row = jnp.where(fwd_zone, middle - 1, middle)
    to_row = jnp.where(fwd_zone, middle, middle - 1)
    detour = jnp.logical_and(zone, row == from_row)
    detour_end = jnp.logical_and(zone, row == to_row)
    relays = jnp.logical_and(zone, row == relay_row)

    barrier = pltpu.get_barrier_semaphore()
    sides = (
        (has_north, (row - 1, col)),
        (has_south, (row + 1, col)),
        (has_west, (row, col - 1)),
        (has_east, (row, col + 1)),
        (detour, (relay_row, partner)),
        (detour_end, (relay_row, partner)),
        (relays, (from_row, partner)),
        (relays, (to_row, partner)),
    )
    count = 0
    for present, where in sides:
        count = count + present.astype(jnp.int32)

        @pl.when(present)
        def _(where=where):
            pl.semaphore_signal(barrier, inc=1, device_id=where, device_id_type=MESH)

    for present, ref in ((has_north, north_in), (has_west, west_in), (has_south, south_in), (has_east, east_in)):
        @pl.when(jnp.logical_not(present))
        def _(ref=ref):
            ref[...] = jnp.zeros_like(ref)

    shots = batches * batch
    pos_all[...] = jnp.transpose(jnp.broadcast_to(pos_ref[0], (128, shots)))
    amp_all[...] = jnp.transpose(jnp.broadcast_to(amp_ref[0], (128, shots)))

    def split(value, high_ref, low_ref):
        high = value.astype(jnp.bfloat16)
        high_ref[...] = high
        low_ref[...] = (value - high.astype(jnp.float32)).astype(jnp.bfloat16)

    def link(kind, b):
        src, dst, where = (
            (south_out, north_in, (row + 1, col)),
            (east_out, west_in, (row, col + 1)),
            (north_out, south_in, (row - 1, col)),
            (west_out, east_in, (row, col - 1)),
        )[kind]
        return pltpu.make_async_remote_copy(
            src_ref=src.at[b], dst_ref=dst.at[b],
            send_sem=send_sem.at[kind, b], recv_sem=recv_sem.at[kind, b],
            device_id=where, device_id_type=MESH,
        )

    def leave(kind, b):
        return pltpu.make_async_remote_copy(
            src_ref=(south_out, None, north_out)[kind].at[b], dst_ref=passing.at[b],
            send_sem=send_sem.at[kind, b], recv_sem=pass_sem.at[b],
            device_id=(relay_row, partner), device_id_type=MESH,
        )

    def onward(kind, b):
        return pltpu.make_async_remote_copy(
            src_ref=passing.at[b], dst_ref=(north_in, None, south_in)[kind].at[b],
            send_sem=onward_sem.at[b], recv_sem=recv_sem.at[kind, b],
            device_id=(to_row, partner), device_id_type=MESH,
        )

    def put(kind, b, present):
        if kind % 2:
            @pl.when(present)
            def _():
                link(kind, b).start()
            return

        around = jnp.logical_and(detour, (adj_zone if kind else fwd_zone))

        @pl.when(jnp.logical_and(present, jnp.logical_not(around)))
        def _():
            link(kind, b).start()

        @pl.when(around)
        def _():
            leave(kind, b).start()

    def relay(b):
        for kind, here in ((0, fwd_zone), (2, adj_zone)):
            @pl.when(here)
            def _(kind=kind):
                leave(kind, b).wait_recv()
                onward(kind, b).start()

    def product(both, high, adjoint):
        wide, narrow = (hi_turned, lo_turned) if adjoint else (hi_ref, lo_ref)
        first = jnp.dot(both, wide[...], preferred_element_type=jnp.float32)
        second = jnp.dot(high, narrow[...], preferred_element_type=jnp.float32)
        return first[:batch] + (first[batch:] + second)

    def source(b, width, offset):
        at = pl.ds(pl.multiple_of(b * batch, batch), batch)
        spot, strength = pos_all[at, :], amp_all[at, :]
        lanes = lax.broadcasted_iota(jnp.int32, (batch, 128), 1)
        return jnp.concatenate(
            [jnp.where(lanes + (offset + j) == spot, strength, 0.0) for j in range(0, width, 128)], axis=1
        )

    def corner_cell(b, row_out, col_out, put_row, put_col, row_kind, col_kind):
        row_out[b] = source(b, half, 0)
        col_out[b] = source(b, half, half)

        put(row_kind, b, put_row)
        put(col_kind, b, put_col)

    def cell(b, adjoint, row_in, col_in, got_row, got_col, row_out, col_out, put_row, put_col, row_kind, col_kind):
        @pl.when(got_row)
        def _():
            link(row_kind, b).wait_recv()

        @pl.when(got_col)
        def _():
            link(col_kind, b).wait_recv()

        inputs = jnp.concatenate([row_in[b], col_in[b]], axis=1)
        high = inputs.astype(jnp.bfloat16)
        low = (inputs - high.astype(jnp.float32)).astype(jnp.bfloat16)
        both = jnp.concatenate([high, low], axis=0)
        result = product(both, high, adjoint) + source(b, order, 0)
        row_out[b] = result[:, :half]

        put(row_kind, b, put_row)

        col_out[b] = result[:, half:]

        put(col_kind, b, put_col)

    def reach(r, c):
        return (r * ROW_HOP + (r // 2) * (FAR_HOP - ROW_HOP)
                + ((c + 1) // 2) * CORE_HOP + (c // 2) * CHIP_HOP)

    far_end = reach(rows - 1, cols - 1)
    lead_fwd = reach(row, col)
    lead_adj = far_end - lead_fwd
    lead_pass = RELAY_HOP + jnp.where(fwd_zone, reach(from_row, partner), far_end - reach(from_row, partner))
    first_cell = jnp.logical_not(jnp.logical_or(has_north, has_west))
    last_cell = jnp.logical_not(jnp.logical_or(has_south, has_east))

    corner = jnp.logical_or(first_cell, last_cell)

    @pl.when(corner)
    def _():
        pl.semaphore_wait(barrier, count)

    @pl.when(first_cell)
    def _():
        lax.fori_loop(0, batches, lambda b, carry: (corner_cell(
            b, south_out, east_out, has_south, has_east, 0, 1), carry)[1], 0)

    @pl.when(last_cell)
    def _():
        lax.fori_loop(0, batches, lambda b, carry: (corner_cell(
            b, north_out, west_out, has_north, has_west, 2, 3), carry)[1], 0)

    near_first, near_last = row + col == 1, row + col == rows + cols - 3
    adj_first = lead_adj < lead_fwd

    def plain():
        split(op_f32[...], hi_ref, lo_ref)

    def turn():
        split(jnp.transpose(op_f32[...]), hi_turned, lo_turned)

    load.wait()
    pl.when(adj_first)(turn)
    pl.when(jnp.logical_not(near_last))(plain)
    pl.when(jnp.logical_not(jnp.logical_or(adj_first, near_first)))(turn)

    @pl.when(jnp.logical_not(corner))
    def _():
        pl.semaphore_wait(barrier, count)

    def tick(step, carry):
        fwd, adj, passed = carry
        fwd_next = jnp.logical_and(
            fwd < batches,
            jnp.logical_or(adj >= batches, lead_fwd + fwd * PERIOD <= lead_adj + adj * PERIOD),
        )
        now = jnp.where(fwd_next, lead_fwd + fwd * PERIOD, lead_adj + adj * PERIOD)
        pass_next = jnp.logical_and(
            passed < batches,
            jnp.logical_or(fwd + adj >= 2 * batches, lead_pass + passed * PERIOD <= now),
        )
        fwd_now = jnp.logical_and(fwd_next, jnp.logical_not(pass_next))
        adj_now = jnp.logical_not(jnp.logical_or(fwd_next, pass_next))

        pl.when(jnp.logical_and(near_first, step == batches))(turn)
        pl.when(jnp.logical_and(near_last, step == batches))(plain)

        @pl.when(pass_next)
        def _():
            relay(passed)

        @pl.when(jnp.logical_and(fwd_now, jnp.logical_not(first_cell)))
        def _():
            cell(fwd, False, north_in, west_in, has_north, has_west,
                 south_out, east_out, has_south, has_east, 0, 1)

        @pl.when(jnp.logical_and(adj_now, jnp.logical_not(last_cell)))
        def _():
            cell(adj, True, south_in, east_in, has_south, has_east,
                 north_out, west_out, has_north, has_west, 2, 3)

        done = jnp.where(fwd_next, fwd, adj)

        @pl.when(jnp.logical_or(jnp.logical_and(fwd_now, fwd < adj), jnp.logical_and(adj_now, adj < fwd)))
        def _():
            at = pl.ds(pl.multiple_of(done * batch, batch), batch)
            out_ref[0, 0, at, :half] = south_out[done] + north_out[done]
            out_ref[0, 0, at, half:] = east_out[done] + west_out[done]

        return fwd + fwd_now.astype(jnp.int32), adj + adj_now.astype(jnp.int32), passed + pass_next.astype(jnp.int32)

    start_pass = jnp.where(relays, 0, batches)
    lax.fori_loop(0, 3 * batches - start_pass, tick, (jnp.int32(0), jnp.int32(0), start_pass))

    def drain(b, carry):
        for kind, present in enumerate((has_south, has_east, has_north, has_west)):
            @pl.when(present)
            def _(kind=kind):
                link(kind, b).wait_send()

        @pl.when(relays)
        def _():
            onward(0, b).wait_send()

        return carry

    lax.fori_loop(0, batches, drain, 0)


def local(rows, cols, operators, positions, amplitudes):
    order = operators.shape[-1]
    shots = positions.shape[-1]
    half = order // 2
    batches = shots // BATCH
    slots = pltpu.VMEM((batches, BATCH, half), jnp.float32)
    return pl.pallas_call(
        functools.partial(kernel, rows, cols),
        out_shape=jax.ShapeDtypeStruct((1, 1, shots, order), jnp.float32),
        in_specs=[
            pl.BlockSpec(memory_space=pltpu.HBM),
            pl.BlockSpec(memory_space=pltpu.VMEM),
            pl.BlockSpec(memory_space=pltpu.VMEM),
        ],
        out_specs=pl.BlockSpec(memory_space=pltpu.VMEM),
        scratch_shapes=[
            pltpu.VMEM((order, order), jnp.float32),
            pltpu.VMEM((order, order), jnp.bfloat16),
            pltpu.VMEM((order, order), jnp.bfloat16),
            pltpu.VMEM((order, order), jnp.bfloat16),
            pltpu.VMEM((order, order), jnp.bfloat16),
            pltpu.VMEM((shots, 128), jnp.int32),
            pltpu.VMEM((shots, 128), jnp.float32),
            slots, slots, slots, slots,
            slots, slots, slots, slots, slots,
            pltpu.SemaphoreType.DMA,
            pltpu.SemaphoreType.DMA((4, batches)),
            pltpu.SemaphoreType.DMA((4, batches)),
            pltpu.SemaphoreType.DMA((batches,)),
            pltpu.SemaphoreType.DMA((batches,)),
        ],
        compiler_params=pltpu.CompilerParams(collective_id=0, has_side_effects=True, vmem_limit_bytes=52 << 20),
    )(operators, positions, amplitudes)


def solution(mesh):
    in_specs = (P("row", "col", None, None), P("row", "col", None), P("row", "col", None))
    out_specs = P("row", "col", None, None)
    body = functools.partial(local, mesh.shape["row"], mesh.shape["col"])
    return jax.shard_map(body, mesh=mesh, in_specs=in_specs, out_specs=out_specs, check_vma=False)
```

```python
import functools

import jax
import jax.numpy as jnp
from jax import lax
from jax.experimental import pallas as pl
from jax.experimental.pallas import tpu as pltpu
from jax.sharding import PartitionSpec as P

BATCH = 32
CORE_HOP, CHIP_HOP, ROW_HOP, FAR_HOP, RELAY_HOP, PERIOD = 12, 28, 32, 60, 32, 5
MESH = pl.DeviceIdType.MESH


def kernel(
    rows, cols, op_hbm, pos_hbm, amp_hbm, out_ref,
    pos_ref, amp_ref, op_f32, hi_ref, lo_ref, hi_turned, lo_turned, pos_all, amp_all,
    north_in, west_in, south_in, east_in,
    south_out, east_out, north_out, west_out, passing,
    pos_sem, amp_sem, op_sem, send_sem, recv_sem, pass_sem, onward_sem,
):
    row = lax.axis_index("row")
    col = lax.axis_index("col")
    batches, batch, half = north_in.shape
    order = 2 * half
    has_north, has_south = row > 0, row < rows - 1
    has_west, has_east = col > 0, col < cols - 1

    load_pos = pltpu.make_async_copy(pos_hbm, pos_ref, pos_sem)
    load_amp = pltpu.make_async_copy(amp_hbm, amp_ref, amp_sem)
    load = pltpu.make_async_copy(op_hbm.at[0, 0], op_f32, op_sem)
    load_pos.start()
    load_amp.start()
    load.start()

    middle, chip = rows // 2, cols // 4
    partner = col + 1 - 2 * (col % 2)
    fwd_zone, adj_zone = col // 2 == chip, col // 2 == chip - 1
    zone = jnp.logical_or(fwd_zone, adj_zone)
    relay_row = jnp.where(fwd_zone, rows - 1, 0)
    from_row = jnp.where(fwd_zone, middle - 1, middle)
    to_row = jnp.where(fwd_zone, middle, middle - 1)
    detour = jnp.logical_and(zone, row == from_row)
    detour_end = jnp.logical_and(zone, row == to_row)
    relays = jnp.logical_and(zone, row == relay_row)

    barrier = pltpu.get_barrier_semaphore()
    sides = (
        (has_north, (row - 1, col)),
        (has_south, (row + 1, col)),
        (has_west, (row, col - 1)),
        (has_east, (row, col + 1)),
        (detour, (relay_row, partner)),
        (detour_end, (relay_row, partner)),
        (relays, (from_row, partner)),
        (relays, (to_row, partner)),
    )
    count = 0
    for present, where in sides:
        count = count + present.astype(jnp.int32)

        @pl.when(present)
        def _(where=where):
            pl.semaphore_signal(barrier, inc=1, device_id=where, device_id_type=MESH)

    for present, ref in ((has_north, north_in), (has_west, west_in), (has_south, south_in), (has_east, east_in)):
        @pl.when(jnp.logical_not(present))
        def _(ref=ref):
            ref[...] = jnp.zeros_like(ref)

    shots = batches * batch
    load_pos.wait()
    load_amp.wait()
    pos_all[...] = jnp.transpose(jnp.broadcast_to(pos_ref[0], (128, shots)))
    amp_all[...] = jnp.transpose(jnp.broadcast_to(amp_ref[0], (128, shots)))

    def split(value, high_ref, low_ref):
        high = value.astype(jnp.bfloat16)
        high_ref[...] = high
        low_ref[...] = (value - high.astype(jnp.float32)).astype(jnp.bfloat16)

    def link(kind, b):
        src, dst, where = (
            (south_out, north_in, (row + 1, col)),
            (east_out, west_in, (row, col + 1)),
            (north_out, south_in, (row - 1, col)),
            (west_out, east_in, (row, col - 1)),
        )[kind]
        return pltpu.make_async_remote_copy(
            src_ref=src.at[b], dst_ref=dst.at[b],
            send_sem=send_sem.at[kind, b], recv_sem=recv_sem.at[kind, b],
            device_id=where, device_id_type=MESH,
        )

    def leave(kind, b):
        return pltpu.make_async_remote_copy(
            src_ref=(south_out, None, north_out)[kind].at[b], dst_ref=passing.at[b],
            send_sem=send_sem.at[kind, b], recv_sem=pass_sem.at[b],
            device_id=(relay_row, partner), device_id_type=MESH,
        )

    def onward(kind, b):
        return pltpu.make_async_remote_copy(
            src_ref=passing.at[b], dst_ref=(north_in, None, south_in)[kind].at[b],
            send_sem=onward_sem.at[b], recv_sem=recv_sem.at[kind, b],
            device_id=(to_row, partner), device_id_type=MESH,
        )

    def put(kind, b, present):
        if kind % 2:
            @pl.when(present)
            def _():
                link(kind, b).start()
            return

        around = jnp.logical_and(detour, (adj_zone if kind else fwd_zone))

        @pl.when(jnp.logical_and(present, jnp.logical_not(around)))
        def _():
            link(kind, b).start()

        @pl.when(around)
        def _():
            leave(kind, b).start()

    def relay(b):
        for kind, here in ((0, fwd_zone), (2, adj_zone)):
            @pl.when(here)
            def _(kind=kind):
                leave(kind, b).wait_recv()
                onward(kind, b).start()

    def product(both, high, adjoint):
        wide, narrow = (hi_turned, lo_turned) if adjoint else (hi_ref, lo_ref)
        first = jnp.dot(both, wide[...], preferred_element_type=jnp.float32)
        second = jnp.dot(high, narrow[...], preferred_element_type=jnp.float32)
        return first[:batch] + (first[batch:] + second)

    def source(b, width, offset):
        at = pl.ds(pl.multiple_of(b * batch, batch), batch)
        spot, strength = pos_all[at, :], amp_all[at, :]
        lanes = lax.broadcasted_iota(jnp.int32, (batch, 128), 1)
        return jnp.concatenate(
            [jnp.where(lanes + (offset + j) == spot, strength, 0.0) for j in range(0, width, 128)], axis=1
        )

    def corner_cell(b, row_out, col_out, put_row, put_col, row_kind, col_kind):
        row_out[b] = source(b, half, 0)
        col_out[b] = source(b, half, half)

        put(row_kind, b, put_row)
        put(col_kind, b, put_col)

    def cell(b, adjoint, row_in, col_in, got_row, got_col, row_out, col_out, put_row, put_col, row_kind, col_kind):
        @pl.when(got_row)
        def _():
            link(row_kind, b).wait_recv()

        @pl.when(got_col)
        def _():
            link(col_kind, b).wait_recv()

        inputs = jnp.concatenate([row_in[b], col_in[b]], axis=1)
        high = inputs.astype(jnp.bfloat16)
        low = (inputs - high.astype(jnp.float32)).astype(jnp.bfloat16)
        both = jnp.concatenate([high, low], axis=0)
        result = product(both, high, adjoint) + source(b, order, 0)
        row_out[b] = result[:, :half]

        put(row_kind, b, put_row)

        col_out[b] = result[:, half:]

        put(col_kind, b, put_col)

    def reach(r, c):
        return (r * ROW_HOP + (r // 2) * (FAR_HOP - ROW_HOP)
                + ((c + 1) // 2) * CORE_HOP + (c // 2) * CHIP_HOP)

    far_end = reach(rows - 1, cols - 1)
    lead_fwd = reach(row, col)
    lead_adj = far_end - lead_fwd
    lead_pass = RELAY_HOP + jnp.where(fwd_zone, reach(from_row, partner), far_end - reach(from_row, partner))
    first_cell = jnp.logical_not(jnp.logical_or(has_north, has_west))
    last_cell = jnp.logical_not(jnp.logical_or(has_south, has_east))

    corner = jnp.logical_or(first_cell, last_cell)

    @pl.when(corner)
    def _():
        pl.semaphore_wait(barrier, count)

    @pl.when(first_cell)
    def _():
        lax.fori_loop(0, batches, lambda b, carry: (corner_cell(
            b, south_out, east_out, has_south, has_east, 0, 1), carry)[1], 0)

    @pl.when(last_cell)
    def _():
        lax.fori_loop(0, batches, lambda b, carry: (corner_cell(
            b, north_out, west_out, has_north, has_west, 2, 3), carry)[1], 0)

    near_first, near_last = row + col == 1, row + col == rows + cols - 3
    adj_first = lead_adj < lead_fwd

    def plain():
        split(op_f32[...], hi_ref, lo_ref)

    def turn():
        split(jnp.transpose(op_f32[...]), hi_turned, lo_turned)

    load.wait()
    pl.when(adj_first)(turn)
    pl.when(jnp.logical_not(near_last))(plain)
    pl.when(jnp.logical_not(jnp.logical_or(adj_first, near_first)))(turn)

    @pl.when(jnp.logical_not(corner))
    def _():
        pl.semaphore_wait(barrier, count)

    def tick(step, carry):
        fwd, adj, passed = carry
        fwd_next = jnp.logical_and(
            fwd < batches,
            jnp.logical_or(adj >= batches, lead_fwd + fwd * PERIOD <= lead_adj + adj * PERIOD),
        )
        now = jnp.where(fwd_next, lead_fwd + fwd * PERIOD, lead_adj + adj * PERIOD)
        pass_next = jnp.logical_and(
            passed < batches,
            jnp.logical_or(fwd + adj >= 2 * batches, lead_pass + passed * PERIOD <= now),
        )
        fwd_now = jnp.logical_and(fwd_next, jnp.logical_not(pass_next))
        adj_now = jnp.logical_not(jnp.logical_or(fwd_next, pass_next))

        pl.when(jnp.logical_and(near_first, step == batches))(turn)
        pl.when(jnp.logical_and(near_last, step == batches))(plain)

        @pl.when(pass_next)
        def _():
            relay(passed)

        @pl.when(jnp.logical_and(fwd_now, jnp.logical_not(first_cell)))
        def _():
            cell(fwd, False, north_in, west_in, has_north, has_west,
                 south_out, east_out, has_south, has_east, 0, 1)

        @pl.when(jnp.logical_and(adj_now, jnp.logical_not(last_cell)))
        def _():
            cell(adj, True, south_in, east_in, has_south, has_east,
                 north_out, west_out, has_north, has_west, 2, 3)

        done = jnp.where(fwd_next, fwd, adj)

        @pl.when(jnp.logical_or(jnp.logical_and(fwd_now, fwd < adj), jnp.logical_and(adj_now, adj < fwd)))
        def _():
            at = pl.ds(pl.multiple_of(done * batch, batch), batch)
            out_ref[0, 0, at, :half] = south_out[done] + north_out[done]
            out_ref[0, 0, at, half:] = east_out[done] + west_out[done]

        return fwd + fwd_now.astype(jnp.int32), adj + adj_now.astype(jnp.int32), passed + pass_next.astype(jnp.int32)

    start_pass = jnp.where(relays, 0, batches)
    lax.fori_loop(0, 3 * batches - start_pass, tick, (jnp.int32(0), jnp.int32(0), start_pass))

    def drain(b, carry):
        for kind, present in enumerate((has_south, has_east, has_north, has_west)):
            @pl.when(present)
            def _(kind=kind):
                link(kind, b).wait_send()

        @pl.when(relays)
        def _():
            onward(0, b).wait_send()

        return carry

    lax.fori_loop(0, batches, drain, 0)


def local(rows, cols, operators, positions, amplitudes):
    order = operators.shape[-1]
    shots = positions.shape[-1]
    half = order // 2
    batches = shots // BATCH
    slots = pltpu.VMEM((batches, BATCH, half), jnp.float32)
    return pl.pallas_call(
        functools.partial(kernel, rows, cols),
        out_shape=jax.ShapeDtypeStruct((1, 1, shots, order), jnp.float32),
        in_specs=[
            pl.BlockSpec(memory_space=pltpu.HBM),
            pl.BlockSpec(memory_space=pltpu.HBM),
            pl.BlockSpec(memory_space=pltpu.HBM),
        ],
        out_specs=pl.BlockSpec(memory_space=pltpu.VMEM),
        scratch_shapes=[
            pltpu.VMEM((1, 1, shots), jnp.int32),
            pltpu.VMEM((1, 1, shots), jnp.float32),
            pltpu.VMEM((order, order), jnp.float32),
            pltpu.VMEM((order, order), jnp.bfloat16),
            pltpu.VMEM((order, order), jnp.bfloat16),
            pltpu.VMEM((order, order), jnp.bfloat16),
            pltpu.VMEM((order, order), jnp.bfloat16),
            pltpu.VMEM((shots, 128), jnp.int32),
            pltpu.VMEM((shots, 128), jnp.float32),
            slots, slots, slots, slots,
            slots, slots, slots, slots, slots,
            pltpu.SemaphoreType.DMA,
            pltpu.SemaphoreType.DMA,
            pltpu.SemaphoreType.DMA,
            pltpu.SemaphoreType.DMA((4, batches)),
            pltpu.SemaphoreType.DMA((4, batches)),
            pltpu.SemaphoreType.DMA((batches,)),
            pltpu.SemaphoreType.DMA((batches,)),
        ],
        compiler_params=pltpu.CompilerParams(collective_id=0, has_side_effects=True, vmem_limit_bytes=52 << 20),
    )(*(pltpu.with_memory_space_constraint(x, pltpu.HBM) for x in (operators, positions, amplitudes)))


def solution(mesh):
    in_specs = (P("row", "col", None, None), P("row", "col", None), P("row", "col", None))
    out_specs = P("row", "col", None, None)
    body = functools.partial(local, mesh.shape["row"], mesh.shape["col"])
    return jax.shard_map(body, mesh=mesh, in_specs=in_specs, out_specs=out_specs, check_vma=False)
```

```python
import functools

import jax
import jax.numpy as jnp
from jax import lax
from jax.experimental import pallas as pl
from jax.experimental.pallas import tpu as pltpu
from jax.sharding import PartitionSpec as P

BATCH = 32
CORE_HOP, CHIP_HOP, ROW_HOP, FAR_HOP, RELAY_HOP, PERIOD = 15, 32, 36, 50, 27, 5
DETOURS = 6
MESH = pl.DeviceIdType.MESH


def kernel(
    rows, cols, op_hbm, pos_hbm, amp_hbm, out_ref,
    pos_ref, amp_ref, op_f32, hi_ref, lo_ref, hi_turned, lo_turned, pos_all, amp_all,
    north_in, west_in, south_in, east_in,
    south_out, east_out, north_out, west_out, passing,
    pos_sem, amp_sem, op_sem, send_sem, recv_sem, pass_sem, onward_sem,
):
    row = lax.axis_index("row")
    col = lax.axis_index("col")
    batches, batch, half = north_in.shape
    order = 2 * half
    detours = batches * DETOURS // 8
    has_north, has_south = row > 0, row < rows - 1
    has_west, has_east = col > 0, col < cols - 1

    load_pos = pltpu.make_async_copy(pos_hbm, pos_ref, pos_sem)
    load_amp = pltpu.make_async_copy(amp_hbm, amp_ref, amp_sem)
    load = pltpu.make_async_copy(op_hbm.at[0, 0], op_f32, op_sem)
    load_pos.start()
    load_amp.start()
    load.start()

    middle, chip = rows // 2, cols // 4
    partner = col + 1 - 2 * (col % 2)
    fwd_zone, adj_zone = col // 2 == chip, col // 2 == chip - 1
    zone = jnp.logical_or(fwd_zone, adj_zone)
    relay_row = jnp.where(fwd_zone, rows - 1, 0)
    from_row = jnp.where(fwd_zone, middle - 1, middle)
    to_row = jnp.where(fwd_zone, middle, middle - 1)
    detour = jnp.logical_and(zone, row == from_row)
    detour_end = jnp.logical_and(zone, row == to_row)
    relays = jnp.logical_and(zone, row == relay_row)

    barrier = pltpu.get_barrier_semaphore()
    sides = (
        (has_north, (row - 1, col)),
        (has_south, (row + 1, col)),
        (has_west, (row, col - 1)),
        (has_east, (row, col + 1)),
        (detour, (relay_row, partner)),
        (detour_end, (relay_row, partner)),
        (relays, (from_row, partner)),
        (relays, (to_row, partner)),
    )
    count = 0
    for present, where in sides:
        count = count + present.astype(jnp.int32)

        @pl.when(present)
        def _(where=where):
            pl.semaphore_signal(barrier, inc=1, device_id=where, device_id_type=MESH)

    for present, ref in ((has_north, north_in), (has_west, west_in), (has_south, south_in), (has_east, east_in)):
        @pl.when(jnp.logical_not(present))
        def _(ref=ref):
            ref[...] = jnp.zeros_like(ref)

    shots = batches * batch
    load_pos.wait()
    load_amp.wait()
    pos_all[...] = jnp.transpose(jnp.broadcast_to(pos_ref[0], (128, shots)))
    amp_all[...] = jnp.transpose(jnp.broadcast_to(amp_ref[0], (128, shots)))

    def split(value, high_ref, low_ref):
        high = value.astype(jnp.bfloat16)
        high_ref[...] = high
        low_ref[...] = (value - high.astype(jnp.float32)).astype(jnp.bfloat16)

    def link(kind, b):
        src, dst, where = (
            (south_out, north_in, (row + 1, col)),
            (east_out, west_in, (row, col + 1)),
            (north_out, south_in, (row - 1, col)),
            (west_out, east_in, (row, col - 1)),
        )[kind]
        return pltpu.make_async_remote_copy(
            src_ref=src.at[b], dst_ref=dst.at[b],
            send_sem=send_sem.at[kind, b], recv_sem=recv_sem.at[kind, b],
            device_id=where, device_id_type=MESH,
        )

    def leave(kind, b):
        return pltpu.make_async_remote_copy(
            src_ref=(south_out, None, north_out)[kind].at[b], dst_ref=passing.at[b],
            send_sem=send_sem.at[kind, b], recv_sem=pass_sem.at[b],
            device_id=(relay_row, partner), device_id_type=MESH,
        )

    def onward(kind, b):
        return pltpu.make_async_remote_copy(
            src_ref=passing.at[b], dst_ref=(north_in, None, south_in)[kind].at[b],
            send_sem=onward_sem.at[b], recv_sem=recv_sem.at[kind, b],
            device_id=(to_row, partner), device_id_type=MESH,
        )

    def put(kind, b, present):
        if kind % 2:
            @pl.when(present)
            def _():
                link(kind, b).start()
            return

        around = jnp.logical_and(jnp.logical_and(detour, b < detours), (adj_zone if kind else fwd_zone))

        @pl.when(jnp.logical_and(present, jnp.logical_not(around)))
        def _():
            link(kind, b).start()

        @pl.when(around)
        def _():
            leave(kind, b).start()

    def relay(b):
        for kind, here in ((0, fwd_zone), (2, adj_zone)):
            @pl.when(here)
            def _(kind=kind):
                leave(kind, b).wait_recv()
                onward(kind, b).start()

    def product(both, high, adjoint):
        wide, narrow = (hi_turned, lo_turned) if adjoint else (hi_ref, lo_ref)
        first = jnp.dot(both, wide[...], preferred_element_type=jnp.float32)
        second = jnp.dot(high, narrow[...], preferred_element_type=jnp.float32)
        return first[:batch] + (first[batch:] + second)

    def source(b, width, offset):
        at = pl.ds(pl.multiple_of(b * batch, batch), batch)
        spot, strength = pos_all[at, :], amp_all[at, :]
        lanes = lax.broadcasted_iota(jnp.int32, (batch, 128), 1)
        return jnp.concatenate(
            [jnp.where(lanes + (offset + j) == spot, strength, 0.0) for j in range(0, width, 128)], axis=1
        )

    def corner_cell(b, row_out, col_out, put_row, put_col, row_kind, col_kind):
        row_out[b] = source(b, half, 0)
        col_out[b] = source(b, half, half)

        put(row_kind, b, put_row)
        put(col_kind, b, put_col)

    def cell(b, adjoint, row_in, col_in, got_row, got_col, row_out, col_out, put_row, put_col, row_kind, col_kind):
        @pl.when(got_row)
        def _():
            link(row_kind, b).wait_recv()

        @pl.when(got_col)
        def _():
            link(col_kind, b).wait_recv()

        inputs = jnp.concatenate([row_in[b], col_in[b]], axis=1)
        high = inputs.astype(jnp.bfloat16)
        low = (inputs - high.astype(jnp.float32)).astype(jnp.bfloat16)
        both = jnp.concatenate([high, low], axis=0)
        result = product(both, high, adjoint) + source(b, order, 0)
        row_out[b] = result[:, :half]

        put(row_kind, b, put_row)

        col_out[b] = result[:, half:]

        put(col_kind, b, put_col)

    def reach(r, c):
        return (r * ROW_HOP + (r // 2) * (FAR_HOP - ROW_HOP)
                + ((c + 1) // 2) * CORE_HOP + (c // 2) * CHIP_HOP)

    far_end = reach(rows - 1, cols - 1)
    lead_fwd = reach(row, col)
    lead_adj = far_end - lead_fwd
    lead_pass = RELAY_HOP + jnp.where(fwd_zone, reach(from_row, partner), far_end - reach(from_row, partner))
    first_cell = jnp.logical_not(jnp.logical_or(has_north, has_west))
    last_cell = jnp.logical_not(jnp.logical_or(has_south, has_east))

    corner = jnp.logical_or(first_cell, last_cell)

    @pl.when(corner)
    def _():
        pl.semaphore_wait(barrier, count)

    @pl.when(first_cell)
    def _():
        lax.fori_loop(0, batches, lambda b, carry: (corner_cell(
            b, south_out, east_out, has_south, has_east, 0, 1), carry)[1], 0)

    @pl.when(last_cell)
    def _():
        lax.fori_loop(0, batches, lambda b, carry: (corner_cell(
            b, north_out, west_out, has_north, has_west, 2, 3), carry)[1], 0)

    near_first, near_last = row + col == 1, row + col == rows + cols - 3
    adj_first = lead_adj < lead_fwd

    def plain():
        split(op_f32[...], hi_ref, lo_ref)

    def turn():
        split(jnp.transpose(op_f32[...]), hi_turned, lo_turned)

    load.wait()
    pl.when(adj_first)(turn)
    pl.when(jnp.logical_not(near_last))(plain)
    pl.when(jnp.logical_not(jnp.logical_or(adj_first, near_first)))(turn)

    @pl.when(jnp.logical_not(corner))
    def _():
        pl.semaphore_wait(barrier, count)

    def tick(step, carry):
        fwd, adj, passed = carry
        fwd_next = jnp.logical_and(
            fwd < batches,
            jnp.logical_or(adj >= batches, lead_fwd + fwd * PERIOD <= lead_adj + adj * PERIOD),
        )
        now = jnp.where(fwd_next, lead_fwd + fwd * PERIOD, lead_adj + adj * PERIOD)
        pass_next = jnp.logical_and(
            passed < detours,
            jnp.logical_or(fwd + adj >= 2 * batches, lead_pass + passed * PERIOD <= now),
        )
        fwd_now = jnp.logical_and(fwd_next, jnp.logical_not(pass_next))
        adj_now = jnp.logical_not(jnp.logical_or(fwd_next, pass_next))

        pl.when(jnp.logical_and(near_first, step == batches))(turn)
        pl.when(jnp.logical_and(near_last, step == batches))(plain)

        @pl.when(pass_next)
        def _():
            relay(passed)

        @pl.when(jnp.logical_and(fwd_now, jnp.logical_not(first_cell)))
        def _():
            cell(fwd, False, north_in, west_in, has_north, has_west,
                 south_out, east_out, has_south, has_east, 0, 1)

        @pl.when(jnp.logical_and(adj_now, jnp.logical_not(last_cell)))
        def _():
            cell(adj, True, south_in, east_in, has_south, has_east,
                 north_out, west_out, has_north, has_west, 2, 3)

        done = jnp.where(fwd_next, fwd, adj)

        @pl.when(jnp.logical_or(jnp.logical_and(fwd_now, fwd < adj), jnp.logical_and(adj_now, adj < fwd)))
        def _():
            at = pl.ds(pl.multiple_of(done * batch, batch), batch)
            out_ref[0, 0, at, :half] = south_out[done] + north_out[done]
            out_ref[0, 0, at, half:] = east_out[done] + west_out[done]

        return fwd + fwd_now.astype(jnp.int32), adj + adj_now.astype(jnp.int32), passed + pass_next.astype(jnp.int32)

    start_pass = jnp.where(relays, 0, detours)
    lax.fori_loop(0, 2 * batches + detours - start_pass, tick, (jnp.int32(0), jnp.int32(0), start_pass))

    def drain(b, carry):
        for kind, present in enumerate((has_south, has_east, has_north, has_west)):
            @pl.when(present)
            def _(kind=kind):
                link(kind, b).wait_send()

        @pl.when(jnp.logical_and(relays, b < detours))
        def _():
            onward(0, b).wait_send()

        return carry

    lax.fori_loop(0, batches, drain, 0)


def local(rows, cols, operators, positions, amplitudes):
    order = operators.shape[-1]
    shots = positions.shape[-1]
    half = order // 2
    batches = shots // BATCH
    slots = pltpu.VMEM((batches, BATCH, half), jnp.float32)
    return pl.pallas_call(
        functools.partial(kernel, rows, cols),
        out_shape=jax.ShapeDtypeStruct((1, 1, shots, order), jnp.float32),
        in_specs=[
            pl.BlockSpec(memory_space=pltpu.HBM),
            pl.BlockSpec(memory_space=pltpu.HBM),
            pl.BlockSpec(memory_space=pltpu.HBM),
        ],
        out_specs=pl.BlockSpec(memory_space=pltpu.VMEM),
        scratch_shapes=[
            pltpu.VMEM((1, 1, shots), jnp.int32),
            pltpu.VMEM((1, 1, shots), jnp.float32),
            pltpu.VMEM((order, order), jnp.float32),
            pltpu.VMEM((order, order), jnp.bfloat16),
            pltpu.VMEM((order, order), jnp.bfloat16),
            pltpu.VMEM((order, order), jnp.bfloat16),
            pltpu.VMEM((order, order), jnp.bfloat16),
            pltpu.VMEM((shots, 128), jnp.int32),
            pltpu.VMEM((shots, 128), jnp.float32),
            slots, slots, slots, slots,
            slots, slots, slots, slots, slots,
            pltpu.SemaphoreType.DMA,
            pltpu.SemaphoreType.DMA,
            pltpu.SemaphoreType.DMA,
            pltpu.SemaphoreType.DMA((4, batches)),
            pltpu.SemaphoreType.DMA((4, batches)),
            pltpu.SemaphoreType.DMA((batches,)),
            pltpu.SemaphoreType.DMA((batches,)),
        ],
        compiler_params=pltpu.CompilerParams(collective_id=0, has_side_effects=True, vmem_limit_bytes=52 << 20),
    )(*(pltpu.with_memory_space_constraint(x, pltpu.HBM) for x in (operators, positions, amplitudes)))


def solution(mesh):
    in_specs = (P("row", "col", None, None), P("row", "col", None), P("row", "col", None))
    out_specs = P("row", "col", None, None)
    body = functools.partial(local, mesh.shape["row"], mesh.shape["col"])
    return jax.shard_map(body, mesh=mesh, in_specs=in_specs, out_specs=out_specs, check_vma=False)
```
